1024 devices in a mesh: ka: 64 (over x_lo, y, core), ga: 16 (over z, x_hi).
Axes of the slice: x: 8 (x_hi: 2, x_lo: 4; x = x_hi * 4 + x_lo), y: 8, z: 8, core: 2. Of those that a mesh axis runs over, the one named last changes fastest.
Arguments:
- band_coefs: bfloat16 [64, 16, 2, 2048], P('ka'), may hold values from -12 to 12
- screening: bfloat16 [1, 2048, 2048], P(None, 'ga'), may hold values from -0.125 to 0.125
- grid_index: int32 [2048], replicated, may hold values from 1 to 4095, as said below
Outputs:
- kernel: float32 [64, 1, 64, 128], P('ka', None, 'ga')
The draws below stay inside these ranges and needn't reach their ends.
Inputs may be any that keep to these rules, and one draw needn't show every extreme that they name: `grid_index`: the 2048 values are distinct flat grid indices x * 16 * 16 + y * 16 + z; the anchor 0 never appears.
All inputs are finite; a program needn't handle non-finite values.
Results may differ from the reference program's by a relative error of at most 0.0049.
Values may be sent and summed in bfloat16 or wider, within the bound.
No kernel may reach another device: no remote copies, remote signals or barrier semaphores. Data moves between devices by JAX's collectives and lax.ppermute only.
A program may use at most 32 MiB of HBM per device.

```python
import math
import jax
import jax.numpy as jnp
from jax import lax

NBND = 8
NG = 2048
NFFT = 16
NS = 1
NK = 64
GRID = 4096


def draw_grid_index(key, part):
    inner = jax.random.permutation(key, GRID - 3)[:NG - 2] + 2
    chosen = jnp.concatenate([inner.astype(jnp.int32), jnp.array([1, GRID - 1], jnp.int32)])
    order = jax.random.permutation(jax.random.fold_in(key, 7), NG)
    return chosen[order].astype(jnp.int32)


def level_of(own_key, shape, split, least, largest):
    loudness = 1.0
    for dim, blocks in split:
        heights = jax.random.uniform(jax.random.fold_in(jax.random.fold_in(own_key, 6), dim), (blocks,), jnp.float32, least / len(split), largest / len(split))
        loudness = loudness * jnp.repeat(jnp.exp(heights), shape[dim] // blocks).reshape((-1,) + (1,) * (len(shape) - 1 - dim))
    return loudness


def bell_draw(key, shape, width, reach, pieces=(), kind=jnp.bfloat16):
    level = level_of(key, shape, pieces, -0.22, 0.18) if pieces else 1.0
    drawn = jax.random.normal(key, shape, jnp.float32) * width * level
    return jnp.minimum(jnp.maximum(drawn, -reach), reach).astype(kind)


def setup_inputs(seed: int = 0) -> dict:
    arg_keys = jax.random.split(jax.random.key(seed), 4)
    band_coefs = bell_draw(arg_keys[0], (NK, 2 * NBND, 2, NG), 2.0, 12.0, ((0, 64),))
    screening = bell_draw(arg_keys[1], (NS, NG, NG), NG ** -0.5, 0.125, ((1, 16),))
    grid_index = draw_grid_index(jax.random.fold_in(arg_keys[3], 71), 0)
    return dict(band_coefs=band_coefs, screening=screening, grid_index=grid_index)


def orbitals(bands, grid_index):
    values = bands.astype(jnp.float32)
    flat = jnp.zeros((bands.shape[0], 2, GRID), jnp.float32).at[:, :, grid_index].set(values)
    field = (flat[:, 0] + 1j * flat[:, 1]).reshape(bands.shape[0], NFFT, NFFT, NFFT)
    return jnp.fft.ifftn(field, axes=(1, 2, 3), norm='ortho')

def densities(first, second, grid_index):
    product = jnp.conj(first)[:, None] * second[None, :]
    product = product.reshape(first.shape[0] * second.shape[0], NFFT, NFFT, NFFT)
    spectrum = jnp.fft.fftn(product, axes=(1, 2, 3), norm='ortho').reshape(product.shape[0], GRID)
    picked = spectrum[:, grid_index]
    return jnp.stack([jnp.real(picked), jnp.imag(picked)], axis=1).astype(jnp.bfloat16)

def reference(band_coefs, screening, grid_index):
    pair_count = NBND * NBND
    scale = 1.0 / math.sqrt(NG)
    blocks = []
    for offset in range(NS):

        def one_point(point):
            here = orbitals(lax.dynamic_index_in_dim(band_coefs, point, 0, False), grid_index)
            other = ((point - offset - 1) % NK).astype(jnp.int32)
            there = orbitals(lax.dynamic_index_in_dim(band_coefs, other, 0, False), grid_index)
            return (densities(here[:NBND], there[:NBND], grid_index), densities(here[NBND:], there[NBND:], grid_index))
        valence, conduction = lax.map(one_point, jnp.arange(NK, dtype=jnp.int32))
        mixed = jnp.dot(valence.reshape(NK * 2 * pair_count, NG), screening[offset].T, preferred_element_type=jnp.float32)
        screened = mixed.astype(jnp.bfloat16).reshape(NK, pair_count, 2, NG)

        def contract(inputs):
            cond, scr = inputs
            left = cond.reshape(pair_count, 2 * NG)
            right_real = scr.reshape(pair_count, 2 * NG)
            right_imag = jnp.concatenate([scr[:, 1], -scr[:, 0]], axis=1)
            real_part = jnp.dot(left, right_real.T, preferred_element_type=jnp.float32)
            imag_part = jnp.dot(left, right_imag.T, preferred_element_type=jnp.float32)
            return jnp.concatenate([real_part, imag_part], axis=1) * scale
        blocks.append(lax.map(contract, (conduction, screened)))
    return jnp.stack(blocks, axis=1)
```

```python
import math

import jax
import jax.numpy as jnp
import numpy as np
from jax import lax
from jax.experimental import pallas as pl
from jax.experimental.pallas import tpu as pltpu
from jax.sharding import PartitionSpec as P

NBND = 8
NG = 2048
NFFT = 16
PLANE = NFFT * NFFT
GRID = NFFT * PLANE
PAIRS = NBND * NBND
STEP = 1.130485
LEVEL = 1.1328025

NT = (((1,), (1,)), ((), ()))
NN = (((1,), (0,)), ((), ()))


def mm(left, right, dims=NN, precision=None):
    return lax.dot_general(left, right, dims, precision=precision, preferred_element_type=jnp.float32)


def plane_table():
    index = np.arange(PLANE)
    phase = np.outer(index // NFFT, index // NFFT) + np.outer(index % NFFT, index % NFFT)
    angle = (phase % NFFT) * (2.0 * math.pi / NFFT)
    return np.stack([np.cos(angle), np.sin(angle)]) * STEP


def radix4(a, b, c, d, sign):
    sr, si = a[0] + c[0], a[1] + c[1]
    dr, di = a[0] - c[0], a[1] - c[1]
    tr, ti = b[0] + d[0], b[1] + d[1]
    er, ei = b[0] - d[0], b[1] - d[1]
    plus = (dr - ei, di + er)
    minus = (dr + ei, di - er)
    first, third = (plus, minus) if sign > 0 else (minus, plus)
    return [(sr + tr, si + ti), first, (sr - tr, si - ti), third]


def turned(value, power, sign):
    if power == 0:
        return value
    re, im = value
    if power == 4:
        return (-im, re) if sign > 0 else (im, -re)
    c = math.cos(2.0 * math.pi * power / NFFT)
    s = sign * math.sin(2.0 * math.pi * power / NFFT)
    if power == 2:
        return ((re - im) * c, (re + im) * c) if sign > 0 else ((re + im) * c, (im - re) * c)
    if power == 6:
        return ((re + im) * c, (im - re) * c) if sign > 0 else ((re - im) * c, (re + im) * c)
    return (re * c - im * s, re * s + im * c)


def sixteen(values, sign):
    inner = [radix4(values[x], values[x + 4], values[x + 8], values[x + 12], sign) for x in range(4)]
    out = [None] * NFFT
    for u in range(4):
        group = radix4(*[turned(inner[x][u], x * u, sign) for x in range(4)], sign)
        for v in range(4):
            out[u + 4 * v] = group[v]
    return out


def selectors(index_ref, plane_ref, masks_ref):
    index = index_ref[...]
    rows = lax.broadcasted_iota(jnp.int32, (PLANE, NG), 0)
    plane_ref[...] = jnp.where(rows == (index & (PLANE - 1)), 1.0, 0.0).astype(jnp.bfloat16)
    levels = lax.broadcasted_iota(jnp.int32, (NFFT, NG), 0)
    masks_ref[...] = jnp.where(levels == (index >> 8), 1.0, 0.0).astype(jnp.bfloat16)


def orbital_kernel(index_ref, coefs_ref, table_ref, psi_ref, plane_ref, masks_ref, spread_ref, field_ref):
    selectors(index_ref, plane_ref, masks_ref)
    bands = 2 * NBND
    half = NFFT * bands
    for part in range(2):
        held = coefs_ref[part]
        for x in range(NFFT):
            spread_ref[pl.ds(part * half + x * bands, bands), :] = held * masks_ref[pl.ds(x, 1), :]
    planes = mm(spread_ref[...], plane_ref[...], NT).astype(jnp.bfloat16)
    field_ref[0] = mm(planes, table_ref[0])
    field_ref[1] = mm(planes, table_ref[1])
    for lane in range(0, PLANE, 128):
        at = pl.ds(lane, 128)
        values = []
        for x in range(NFFT):
            top, low = pl.ds(x * bands, bands), pl.ds(half + x * bands, bands)
            re = field_ref[0, top, at] - field_ref[1, low, at]
            im = field_ref[1, top, at] + field_ref[0, low, at]
            values.append((re, im))
        for u, (re, im) in enumerate(sixteen(values, 1)):
            psi_ref[0, :, pl.ds(u * PLANE + lane, 128)] = re
            psi_ref[1, :, pl.ds(u * PLANE + lane, 128)] = im


def screen_kernel(place_ref, index_ref, own_ref, weights_ref, table_ref, wide_ref, waves_ref,
                  plane_ref, masks_ref, spread_ref, field_ref):
    selectors(index_ref, plane_ref, masks_ref)
    strip = weights_ref.shape[0]
    group = 4

    def some_planes(step, carry):
        for x in range(group):
            mask = masks_ref[pl.ds(step * group + x, 1), :]
            spread_ref[pl.ds(x * strip, strip), :] = weights_ref[...] * mask
        planes = mm(spread_ref[...], plane_ref[...], NT).astype(jnp.bfloat16)
        rows = pl.ds(pl.multiple_of(step * (group * strip), group * strip), group * strip)
        field_ref[0, rows, :] = mm(planes, table_ref[0])
        field_ref[1, rows, :] = mm(planes, table_ref[1])
        return carry

    for step in range(NFFT // group):
        some_planes(step, 0)

    def some_rows(step, carry):
        first = pl.multiple_of(step * 16, 16)
        for lane in range(0, PLANE, 128):
            at = pl.ds(lane, 128)
            values = []
            for x in range(NFFT):
                rows = pl.ds(pl.multiple_of(x * strip + first, 16), 16)
                values.append((field_ref[0, rows, at], -field_ref[1, rows, at]))
            for u, (re, im) in enumerate(sixteen(values, -1)):
                out = pl.ds(u * PLANE + lane, 128)
                wide_ref[pl.ds(first, 16), out] = re.astype(jnp.bfloat16)
                wide_ref[pl.ds(pl.multiple_of(first + strip, 16), 16), out] = im.astype(jnp.bfloat16)
        return carry

    lax.fori_loop(0, strip // 16, some_rows, 0)

    chosen = plane_ref[:, pl.ds(pl.multiple_of(place_ref[0] * strip, strip), strip)]
    cos_plane = mm(table_ref[0], chosen)
    sin_plane = mm(table_ref[1], chosen)
    level = own_ref[...] >> 8
    turn = (level * lax.broadcasted_iota(jnp.int32, (NFFT, strip), 0)) & (NFFT - 1)
    angle = turn.astype(jnp.float32) * (2.0 * math.pi / NFFT)
    cos_line = jnp.cos(angle)
    sin_line = jnp.sin(angle)
    for u in range(NFFT):
        c, s = cos_line[u : u + 1, :], sin_line[u : u + 1, :]
        rows = pl.ds(u * PLANE, PLANE)
        waves_ref[rows, pl.ds(0, strip)] = (cos_plane * c - sin_plane * s).astype(jnp.bfloat16)
        waves_ref[rows, pl.ds(strip, strip)] = (-(sin_plane * c + cos_plane * s)).astype(jnp.bfloat16)


def contract_kernel(scale, here_ref, there_ref, wide_ref, waves_ref, out_ref, valence_ref, conduction_ref):
    strip = wide_ref.shape[0] // 2
    chunk = 512
    for lane in range(0, GRID, chunk):
        at = pl.ds(lane, chunk)
        for first, target in ((0, valence_ref), (NBND, conduction_ref)):
            br = there_ref[0, pl.ds(first, NBND), at]
            bi = there_ref[1, pl.ds(first, NBND), at]
            for v in range(0, NBND, 2):
                re, im = [], []
                for band in (first + v, first + v + 1):
                    ar = here_ref[0, pl.ds(band, 1), at]
                    ai = here_ref[1, pl.ds(band, 1), at]
                    re.append(ar * br + ai * bi)
                    im.append(ar * bi - ai * br)
                target[pl.ds(v * NBND, 2 * NBND), at] = jnp.concatenate(re, 0).astype(jnp.bfloat16)
                target[pl.ds(PAIRS + v * NBND, 2 * NBND), at] = jnp.concatenate(im, 0).astype(jnp.bfloat16)

    def joined(block):
        re = block[:PAIRS, :strip] - block[PAIRS:, strip:]
        im = block[:PAIRS, strip:] + block[PAIRS:, :strip]
        return re, im

    sr, si = joined(mm(valence_ref[...], wide_ref[...], NT))
    cr, ci = joined(mm(conduction_ref[...], waves_ref[...]))
    left = jnp.concatenate([cr, ci], 1)
    right = jnp.concatenate([jnp.concatenate([sr, si], 1), jnp.concatenate([si, -sr], 1)], 0)
    out_ref[...] = mm(left, right, NT, lax.Precision.HIGHEST) * scale


def passed_along(value, axis, by):
    size = lax.axis_size(axis)
    return lax.ppermute(value, axis, [(i, (i + by) % size) for i in range(size)])


def called(kernel, shapes, scratch, flops, moved, *args, smem=0):
    specs = [pl.BlockSpec(memory_space=pltpu.SMEM)] * smem
    specs += [pl.BlockSpec(memory_space=pltpu.VMEM)] * (len(args) - smem)
    out_specs = [pl.BlockSpec(memory_space=pltpu.VMEM) for _ in shapes]
    return pl.pallas_call(
        kernel,
        out_shape=shapes,
        in_specs=specs,
        out_specs=out_specs,
        scratch_shapes=scratch,
        cost_estimate=pl.CostEstimate(flops=flops, bytes_accessed=moved, transcendentals=0),
        compiler_params=pltpu.CompilerParams(vmem_limit_bytes=36 * 1024 * 1024),
    )(*args)


def orbitals(index, coefs, table):
    bands = coefs.shape[1]
    shape = jax.ShapeDtypeStruct((2, bands, GRID), jnp.float32)
    scratch = [
        pltpu.VMEM((PLANE, NG), jnp.bfloat16),
        pltpu.VMEM((NFFT, NG), jnp.bfloat16),
        pltpu.VMEM((2 * NFFT * bands, NG), jnp.bfloat16),
        pltpu.VMEM((2, 2 * NFFT * bands, PLANE), jnp.float32),
    ]
    return called(orbital_kernel, [shape], scratch, 10**9, 2**20, index, coefs, table)[0]


def screening_waves(place, index, own, weights, table):
    strip = weights.shape[0]
    shapes = [
        jax.ShapeDtypeStruct((2 * strip, GRID), jnp.bfloat16),
        jax.ShapeDtypeStruct((GRID, 2 * strip), jnp.bfloat16),
    ]
    scratch = [
        pltpu.VMEM((PLANE, NG), jnp.bfloat16),
        pltpu.VMEM((NFFT, NG), jnp.bfloat16),
        pltpu.VMEM((4 * strip, NG), jnp.bfloat16),
        pltpu.VMEM((2, NFFT * strip, PLANE), jnp.float32),
    ]
    return called(screen_kernel, shapes, scratch, 5 * 10**9, 2**23, place, index, own, weights, table, smem=1)


def contracted(here, there, wide, waves, scale):
    shape = jax.ShapeDtypeStruct((PAIRS, 2 * PAIRS), jnp.float32)
    scratch = [pltpu.VMEM((2 * PAIRS, GRID), jnp.bfloat16) for _ in range(2)]

    def kernel(*refs):
        contract_kernel(scale, *refs)

    return called(kernel, [shape], scratch, 10**9, 2**22, here, there, wide, waves)[0]


def body(band_coefs, screening, grid_index):
    width = lax.axis_size("ga")
    place = lax.axis_index("ga").astype(jnp.int32)
    strip = screening.shape[1]
    table = jnp.asarray(plane_table(), jnp.bfloat16)
    index = grid_index.reshape(1, NG)
    coefs = jnp.transpose(band_coefs[0], (1, 0, 2))
    here = orbitals(index, coefs, table)
    there = passed_along(here, "ka", 1)
    own = lax.dynamic_slice_in_dim(index, place * strip, strip, 1)
    wide, waves = screening_waves(place.reshape(1), index, own, screening[0], table)
    scale = 1.0 / (math.sqrt(NG) * (math.sqrt(GRID) * LEVEL) ** 6)
    terms = contracted(here, there, wide, waves, scale)
    rows = terms.shape[0] // width
    pieces = lax.all_to_all(terms.reshape(width, rows, 2 * PAIRS), "ga", 0, 0, tiled=True)
    return jnp.sum(pieces, axis=0)[None, None]


def solution(mesh):
    return jax.shard_map(
        body,
        mesh=mesh,
        in_specs=(P("ka", None, None, None), P(None, "ga", None), P()),
        out_specs=P("ka", None, "ga", None),
        check_vma=False,
    )
```

```python
import math

import jax
import jax.numpy as jnp
import numpy as np
from jax import lax
from jax.experimental import pallas as pl
from jax.experimental.pallas import tpu as pltpu
from jax.sharding import PartitionSpec as P

NBND = 8
NG = 2048
NFFT = 16
PLANE = NFFT * NFFT
GRID = NFFT * PLANE
PAIRS = NBND * NBND
STEP = 1.130485
LEVEL = 1.1328025

NT = (((1,), (1,)), ((), ()))
NN = (((1,), (0,)), ((), ()))


def mm(left, right, dims=NN, precision=None):
    return lax.dot_general(left, right, dims, precision=precision, preferred_element_type=jnp.float32)


def plane_table():
    index = np.arange(PLANE)
    phase = np.outer(index // NFFT, index // NFFT) + np.outer(index % NFFT, index % NFFT)
    angle = (phase % NFFT) * (2.0 * math.pi / NFFT)
    return np.stack([np.cos(angle), np.sin(angle)]) * STEP


def radix4(a, b, c, d, sign):
    sr, si = a[0] + c[0], a[1] + c[1]
    dr, di = a[0] - c[0], a[1] - c[1]
    tr, ti = b[0] + d[0], b[1] + d[1]
    er, ei = b[0] - d[0], b[1] - d[1]
    plus = (dr - ei, di + er)
    minus = (dr + ei, di - er)
    first, third = (plus, minus) if sign > 0 else (minus, plus)
    return [(sr + tr, si + ti), first, (sr - tr, si - ti), third]


def turned(value, power, sign):
    if power == 0:
        return value
    re, im = value
    if power == 4:
        return (-im, re) if sign > 0 else (im, -re)
    c = math.cos(2.0 * math.pi * power / NFFT)
    s = sign * math.sin(2.0 * math.pi * power / NFFT)
    if power == 2:
        return ((re - im) * c, (re + im) * c) if sign > 0 else ((re + im) * c, (im - re) * c)
    if power == 6:
        return ((re + im) * c, (im - re) * c) if sign > 0 else ((re - im) * c, (re + im) * c)
    return (re * c - im * s, re * s + im * c)


def sixteen(values, sign):
    inner = [radix4(values[x], values[x + 4], values[x + 8], values[x + 12], sign) for x in range(4)]
    out = [None] * NFFT
    for u in range(4):
        group = radix4(*[turned(inner[x][u], x * u, sign) for x in range(4)], sign)
        for v in range(4):
            out[u + 4 * v] = group[v]
    return out


def selectors(index_ref, plane_ref, masks_ref):
    index = index_ref[...]
    rows = lax.broadcasted_iota(jnp.int32, (PLANE, NG), 0)
    plane_ref[...] = jnp.where(rows == (index & (PLANE - 1)), 1.0, 0.0).astype(jnp.bfloat16)
    levels = lax.broadcasted_iota(jnp.int32, (NFFT, NG), 0)
    masks_ref[...] = jnp.where(levels == (index >> 8), 1.0, 0.0).astype(jnp.bfloat16)


def fill_orbitals(coefs_ref, table_ref, plane_ref, masks_ref, psi_ref, spread_ref, field_ref, copy=None):
    bands = 2 * NBND
    half = NFFT * bands
    for part in range(2):
        held = coefs_ref[:, part, :]
        for x in range(NFFT):
            spread_ref[pl.ds(part * half + x * bands, bands), :] = held * masks_ref[pl.ds(x, 1), :]
    planes = mm(spread_ref[...], plane_ref[...], NT).astype(jnp.bfloat16)
    if copy is not None:
        copy.wait()
    field_ref[0] = mm(planes, table_ref[0])
    field_ref[1] = mm(planes, table_ref[1])
    for lane in range(0, PLANE, 128):
        at = pl.ds(lane, 128)
        values = []
        for x in range(NFFT):
            top, low = pl.ds(x * bands, bands), pl.ds(half + x * bands, bands)
            re = field_ref[0, top, at] - field_ref[1, low, at]
            im = field_ref[1, top, at] + field_ref[0, low, at]
            values.append((re, im))
        for u, (re, im) in enumerate(sixteen(values, 1)):
            psi_ref[0, :, pl.ds(u * PLANE + lane, 128)] = re
            psi_ref[1, :, pl.ds(u * PLANE + lane, 128)] = im


def prepare_kernel(place_ref, index_hbm, coefs_hbm, weights_hbm, table_hbm,
                   psi_ref, wide_ref, waves_ref, plane_ref, masks_ref,
                   small_ref, small_field_ref, spread_ref, planes_ref, field_ref,
                   index_ref, coefs_ref, weights_ref, table_ref, sems):
    pairs = ((index_hbm, index_ref), (weights_hbm, weights_ref), (table_hbm, table_ref), (coefs_hbm, coefs_ref))
    copies = [pltpu.make_async_copy(source, target, sems.at[i]) for i, (source, target) in enumerate(pairs)]
    for copy in copies:
        copy.start()
    copies[0].wait()
    selectors(index_ref, plane_ref, masks_ref)
    strip = weights_ref.shape[0]
    first_own = pl.multiple_of(place_ref[0] * strip, strip)
    level = index_ref[:, pl.ds(first_own, strip)] >> 8
    turn = (level * lax.broadcasted_iota(jnp.int32, (NFFT, strip), 0)) & (NFFT - 1)
    angle = turn.astype(jnp.float32) * (2.0 * math.pi / NFFT)
    cos_line = jnp.cos(angle)
    sin_line = jnp.sin(angle)
    copies[1].wait()
    copies[2].wait()
    chosen = plane_ref[:, pl.ds(first_own, strip)]
    cos_plane = mm(table_ref[0], chosen)
    sin_plane = mm(table_ref[1], chosen)
    group = 4
    for step in range(NFFT // group):
        for x in range(step * group, (step + 1) * group):
            spread_ref[pl.ds(x * strip, strip), :] = weights_ref[...] * masks_ref[pl.ds(x, 1), :]
        some = pl.ds(step * group * strip, group * strip)
        planes_ref[some, :] = mm(spread_ref[some, :], plane_ref[...], NT).astype(jnp.bfloat16)
        for u in range(step * group, (step + 1) * group):
            c, s = cos_line[u : u + 1, :], sin_line[u : u + 1, :]
            rows = pl.ds(u * PLANE, PLANE)
            waves_ref[rows, pl.ds(0, strip)] = (cos_plane * c - sin_plane * s).astype(jnp.bfloat16)
            waves_ref[rows, pl.ds(strip, strip)] = (-(sin_plane * c + cos_plane * s)).astype(jnp.bfloat16)
    copies[3].wait()
    fill_orbitals(coefs_ref, table_ref, plane_ref, masks_ref, psi_ref, small_ref, small_field_ref)
    field_ref[0] = mm(planes_ref[...], table_ref[0])
    field_ref[1] = mm(planes_ref[...], table_ref[1])

    def some_rows(step, carry):
        first = pl.multiple_of(step * 16, 16)
        for lane in range(0, PLANE, 128):
            at = pl.ds(lane, 128)
            values = []
            for x in range(NFFT):
                rows = pl.ds(pl.multiple_of(x * strip + first, 16), 16)
                values.append((field_ref[0, rows, at], -field_ref[1, rows, at]))
            for u, (re, im) in enumerate(sixteen(values, -1)):
                out = pl.ds(u * PLANE + lane, 128)
                wide_ref[pl.ds(first, 16), out] = re.astype(jnp.bfloat16)
                wide_ref[pl.ds(pl.multiple_of(first + strip, 16), 16), out] = im.astype(jnp.bfloat16)
        return carry

    lax.fori_loop(0, strip // 16, some_rows, 0)


def contract_kernel(scale, coefs_ref, table_hbm, here_ref, wide_ref, waves_ref, plane_ref, masks_ref, out_ref,
                    small_ref, small_field_ref, there_ref, valence_ref, conduction_ref, table_ref, sem):
    copy = pltpu.make_async_copy(table_hbm, table_ref, sem)
    copy.start()
    fill_orbitals(coefs_ref, table_ref, plane_ref, masks_ref, there_ref, small_ref, small_field_ref, copy)
    strip = wide_ref.shape[0] // 2
    chunk = 512
    for lane in range(0, GRID, chunk):
        at = pl.ds(lane, chunk)
        for first, target in ((0, valence_ref), (NBND, conduction_ref)):
            br = there_ref[0, pl.ds(first, NBND), at]
            bi = there_ref[1, pl.ds(first, NBND), at]
            for v in range(0, NBND, 2):
                re, im = [], []
                for band in (first + v, first + v + 1):
                    ar = here_ref[0, pl.ds(band, 1), at]
                    ai = here_ref[1, pl.ds(band, 1), at]
                    re.append(ar * br + ai * bi)
                    im.append(ar * bi - ai * br)
                target[pl.ds(v * NBND, 2 * NBND), at] = jnp.concatenate(re, 0).astype(jnp.bfloat16)
                target[pl.ds(PAIRS + v * NBND, 2 * NBND), at] = jnp.concatenate(im, 0).astype(jnp.bfloat16)

    def joined(block):
        re = block[:PAIRS, :strip] - block[PAIRS:, strip:]
        im = block[:PAIRS, strip:] + block[PAIRS:, :strip]
        return re, im

    sr, si = joined(mm(valence_ref[...], wide_ref[...], NT))
    cr, ci = joined(mm(conduction_ref[...], waves_ref[...]))
    left = jnp.concatenate([cr, ci], 1)
    right = jnp.concatenate([jnp.concatenate([sr, si], 1), jnp.concatenate([si, -sr], 1)], 0)
    out_ref[...] = mm(left, right, NT, lax.Precision.HIGHEST) * scale


def passed_along(value, axis, by):
    size = lax.axis_size(axis)
    return lax.ppermute(value, axis, [(i, (i + by) % size) for i in range(size)])


def called(kernel, shapes, scratch, flops, moved, places, *args):
    spaces = {"s": pltpu.SMEM, "h": pltpu.HBM, "v": pltpu.VMEM}
    args = [pltpu.with_memory_space_constraint(a, pltpu.HBM) if p == "h" else a for a, p in zip(args, places)]
    return pl.pallas_call(
        kernel,
        out_shape=shapes,
        in_specs=[pl.BlockSpec(memory_space=spaces[place]) for place in places],
        out_specs=[pl.BlockSpec(memory_space=pltpu.VMEM) for _ in shapes],
        scratch_shapes=scratch,
        cost_estimate=pl.CostEstimate(flops=flops, bytes_accessed=moved, transcendentals=0),
        compiler_params=pltpu.CompilerParams(vmem_limit_bytes=36 * 1024 * 1024),
    )(*args)


def small_scratch():
    rows = 4 * NBND * NFFT
    return [pltpu.VMEM((rows, NG), jnp.bfloat16), pltpu.VMEM((2, rows, PLANE), jnp.float32)]


def prepared(place, index, coefs, weights, table):
    strip = weights.shape[0]
    shapes = [
        jax.ShapeDtypeStruct((2, 2 * NBND, GRID), jnp.float32),
        jax.ShapeDtypeStruct((2 * strip, GRID), jnp.bfloat16),
        jax.ShapeDtypeStruct((GRID, 2 * strip), jnp.bfloat16),
        jax.ShapeDtypeStruct((PLANE, NG), jnp.bfloat16),
        jax.ShapeDtypeStruct((NFFT, NG), jnp.bfloat16),
    ]
    scratch = small_scratch() + [
        pltpu.VMEM((NFFT * strip, NG), jnp.bfloat16),
        pltpu.VMEM((NFFT * strip, PLANE), jnp.bfloat16),
        pltpu.VMEM((2, NFFT * strip, PLANE), jnp.float32),
    ]
    scratch += [pltpu.VMEM(value.shape, value.dtype) for value in (index, coefs, weights, table)]
    scratch += [pltpu.SemaphoreType.DMA((4,))]
    return called(prepare_kernel, shapes, scratch, 6 * 10**9, 2**23, "shhhh", place, index, coefs, weights, table)


def contracted(coefs, table, here, wide, waves, plane, masks, scale):
    shape = jax.ShapeDtypeStruct((PAIRS, 2 * PAIRS), jnp.float32)
    scratch = small_scratch() + [pltpu.VMEM((2, 2 * NBND, GRID), jnp.float32)]
    scratch += [pltpu.VMEM((2 * PAIRS, GRID), jnp.bfloat16) for _ in range(2)]
    scratch += [pltpu.VMEM(table.shape, table.dtype), pltpu.SemaphoreType.DMA]

    def kernel(*refs):
        contract_kernel(scale, *refs)

    return called(kernel, [shape], scratch, 10**9, 2**22, "vhvvvvv", coefs, table, here, wide, waves, plane, masks)[0]


def body(band_coefs, screening, grid_index):
    width = lax.axis_size("ga")
    place = lax.axis_index("ga").astype(jnp.int32)
    coefs = band_coefs[0]
    moved = passed_along(coefs, "ka", 1)
    table = jnp.asarray(plane_table(), jnp.bfloat16)
    index = grid_index.reshape(1, NG)
    here, wide, waves, plane, masks = prepared(place.reshape(1), index, coefs, screening[0], table)
    scale = 1.0 / (math.sqrt(NG) * (math.sqrt(GRID) * LEVEL) ** 6)
    terms = contracted(moved, table, here, wide, waves, plane, masks, scale)
    rows = terms.shape[0] // width
    pieces = lax.all_to_all(terms.reshape(width, rows, 2 * PAIRS), "ga", 0, 0, tiled=True)
    return jnp.sum(pieces, axis=0)[None, None]


def solution(mesh):
    return jax.shard_map(
        body,
        mesh=mesh,
        in_specs=(P("ka", None, None, None), P(None, "ga", None), P()),
        out_specs=P("ka", None, "ga", None),
        check_vma=False,
    )
```

```python
import math

import jax
import jax.numpy as jnp
import numpy as np
from jax import lax
from jax.experimental import pallas as pl
from jax.experimental.pallas import tpu as pltpu
from jax.sharding import PartitionSpec as P

NBND = 8
NG = 2048
NFFT = 16
PLANE = NFFT * NFFT
GRID = NFFT * PLANE
PAIRS = NBND * NBND
STEP = 1.130485
LEVEL = 1.1328025

NT = (((1,), (1,)), ((), ()))
NN = (((1,), (0,)), ((), ()))


def mm(left, right, dims=NN, precision=None):
    return lax.dot_general(left, right, dims, precision=precision, preferred_element_type=jnp.float32)


def plane_table():
    index = np.arange(PLANE)
    phase = np.outer(index // NFFT, index // NFFT) + np.outer(index % NFFT, index % NFFT)
    angle = (phase % NFFT) * (2.0 * math.pi / NFFT)
    cos, sin = np.cos(angle) * STEP, np.sin(angle) * STEP
    blocks = [np.concatenate([cos[:, at : at + 128], sin[:, at : at + 128]], 1) for at in range(0, PLANE, 128)]
    return np.stack(blocks + [cos, sin])


def radix4(a, b, c, d, sign):
    sr, si = a[0] + c[0], a[1] + c[1]
    dr, di = a[0] - c[0], a[1] - c[1]
    tr, ti = b[0] + d[0], b[1] + d[1]
    er, ei = b[0] - d[0], b[1] - d[1]
    plus = (dr - ei, di + er)
    minus = (dr + ei, di - er)
    first, third = (plus, minus) if sign > 0 else (minus, plus)
    return [(sr + tr, si + ti), first, (sr - tr, si - ti), third]


def turned(value, power, sign):
    if power == 0:
        return value
    re, im = value
    if power == 4:
        return (-im, re) if sign > 0 else (im, -re)
    c = math.cos(2.0 * math.pi * power / NFFT)
    s = sign * math.sin(2.0 * math.pi * power / NFFT)
    if power == 2:
        return ((re - im) * c, (re + im) * c) if sign > 0 else ((re + im) * c, (im - re) * c)
    if power == 6:
        return ((re + im) * c, (im - re) * c) if sign > 0 else ((re - im) * c, (re + im) * c)
    return (re * c - im * s, re * s + im * c)


def sixteen(values, sign):
    inner = [radix4(values[x], values[x + 4], values[x + 8], values[x + 12], sign) for x in range(4)]
    out = [None] * NFFT
    for u in range(4):
        group = radix4(*[turned(inner[x][u], x * u, sign) for x in range(4)], sign)
        for v in range(4):
            out[u + 4 * v] = group[v]
    return out


def selectors(index_ref, plane_ref, masks_ref):
    index = index_ref[...]
    rows = lax.broadcasted_iota(jnp.int32, (PLANE, NG), 0)
    plane_ref[...] = jnp.where(rows == (index & (PLANE - 1)), 1.0, 0.0).astype(jnp.bfloat16)
    levels = lax.broadcasted_iota(jnp.int32, (NFFT, NG), 0)
    masks_ref[...] = jnp.where(levels == (index >> 8), 1.0, 0.0).astype(jnp.bfloat16)


def finish_orbitals(block, field_ref, pitch, base, psi_ref):
    bands = 2 * NBND
    values = []
    for x in range(NFFT):
        top, low = pl.ds(x * pitch + base, bands), pl.ds(x * pitch + base + bands, bands)
        re = field_ref[block, top, pl.ds(0, 128)] - field_ref[block, low, pl.ds(128, 128)]
        im = field_ref[block, top, pl.ds(128, 128)] + field_ref[block, low, pl.ds(0, 128)]
        values.append((re, im))
    for u, (re, im) in enumerate(sixteen(values, 1)):
        at = pl.ds(u * PLANE + block * 128, 128)
        psi_ref[0, :, at] = re
        psi_ref[1, :, at] = im


def spread_orbitals(parts_ref, masks_ref, spread_ref, x, pitch, base):
    bands = 2 * NBND
    for part in range(2):
        rows = pl.ds(x * pitch + base + part * bands, bands)
        spread_ref[rows, :] = parts_ref[part] * masks_ref[pl.ds(x, 1), :]


def fill_orbitals(coefs_ref, table_ref, plane_ref, masks_ref, psi_ref, spread_ref, field_ref, parts_ref):
    for part in range(2):
        parts_ref[part] = coefs_ref[:, part, :]
    for x in range(NFFT):
        spread_orbitals(parts_ref, masks_ref, spread_ref, x, 4 * NBND, 0)
    planes = mm(spread_ref[...], plane_ref[...], NT).astype(jnp.bfloat16)
    for block in range(2):
        field_ref[block] = mm(planes, table_ref[block])
        finish_orbitals(block, field_ref, 4 * NBND, 0, psi_ref)


def prepare_kernel(place_ref, index_hbm, coefs_hbm, weights_hbm, table_hbm,
                   psi_ref, wide_ref, waves_ref, plane_ref, masks_ref, table_ref,
                   spread_ref, planes_ref, field_ref,
                   parts_ref, index_ref, coefs_ref, weights_ref, sems):
    pairs = ((index_hbm, index_ref), (weights_hbm, weights_ref), (table_hbm, table_ref), (coefs_hbm, coefs_ref))
    copies = [pltpu.make_async_copy(source, target, sems.at[i]) for i, (source, target) in enumerate(pairs)]
    for copy in copies:
        copy.start()
    copies[0].wait()
    selectors(index_ref, plane_ref, masks_ref)
    strip = weights_ref.shape[0]
    first_own = pl.multiple_of(place_ref[0] * strip, strip)
    level = index_ref[:, pl.ds(first_own, strip)] >> 8
    turn = (level * lax.broadcasted_iota(jnp.int32, (NFFT, strip), 0)) & (NFFT - 1)
    angle = turn.astype(jnp.float32) * (2.0 * math.pi / NFFT)
    cos_line = jnp.cos(angle)
    sin_line = jnp.sin(angle)
    copies[1].wait()
    copies[2].wait()
    copies[3].wait()
    for part in range(2):
        parts_ref[part] = coefs_ref[:, part, :]
    chosen = plane_ref[:, pl.ds(first_own, strip)]
    cos_plane = mm(table_ref[2], chosen)
    sin_plane = mm(table_ref[3], chosen)
    group = 4
    pitch = strip + 4 * NBND
    for step in range(NFFT // group):
        for x in range(step * group, (step + 1) * group):
            spread_ref[pl.ds(x * pitch, strip), :] = weights_ref[...] * masks_ref[pl.ds(x, 1), :]
            spread_orbitals(parts_ref, masks_ref, spread_ref, x, pitch, strip)
        some = pl.ds(step * group * pitch, group * pitch)
        planes_ref[some, :] = mm(spread_ref[some, :], plane_ref[...], NT).astype(jnp.bfloat16)
        for u in range(step * group, (step + 1) * group):
            c, s = cos_line[u : u + 1, :], sin_line[u : u + 1, :]
            rows = pl.ds(u * PLANE, PLANE)
            waves_ref[rows, pl.ds(0, strip)] = (cos_plane * c - sin_plane * s).astype(jnp.bfloat16)
            waves_ref[rows, pl.ds(strip, strip)] = (-(sin_plane * c + cos_plane * s)).astype(jnp.bfloat16)
    for block in range(2):
        field_ref[block] = mm(planes_ref[...], table_ref[block])
        finish_orbitals(block, field_ref, pitch, strip, psi_ref)
        for first in range(0, strip, 16):
            values = []
            for x in range(NFFT):
                rows = pl.ds(x * pitch + first, 16)
                values.append((field_ref[block, rows, pl.ds(0, 128)], -field_ref[block, rows, pl.ds(128, 128)]))
            for u, (re, im) in enumerate(sixteen(values, -1)):
                out = pl.ds(u * PLANE + block * 128, 128)
                wide_ref[pl.ds(first, 16), out] = re.astype(jnp.bfloat16)
                wide_ref[pl.ds(first + strip, 16), out] = im.astype(jnp.bfloat16)


def contract_kernel(scale, coefs_ref, here_ref, wide_ref, waves_ref, plane_ref, masks_ref, table_ref, out_ref,
                    small_ref, small_field_ref, there_ref, valence_ref, conduction_ref, parts_ref):
    fill_orbitals(coefs_ref, table_ref, plane_ref, masks_ref, there_ref, small_ref, small_field_ref, parts_ref)
    strip = wide_ref.shape[0] // 2
    chunk = 512
    for lane in range(0, GRID, chunk):
        at = pl.ds(lane, chunk)
        for first, target in ((0, valence_ref), (NBND, conduction_ref)):
            br = there_ref[0, pl.ds(first, NBND), at]
            bi = there_ref[1, pl.ds(first, NBND), at]
            for v in range(0, NBND, 2):
                re, im = [], []
                for band in (first + v, first + v + 1):
                    ar = here_ref[0, pl.ds(band, 1), at]
                    ai = here_ref[1, pl.ds(band, 1), at]
                    re.append(ar * br + ai * bi)
                    im.append(ar * bi - ai * br)
                target[pl.ds(v * NBND, 2 * NBND), at] = jnp.concatenate(re, 0).astype(jnp.bfloat16)
                target[pl.ds(PAIRS + v * NBND, 2 * NBND), at] = jnp.concatenate(im, 0).astype(jnp.bfloat16)

    def joined(block):
        re = block[:PAIRS, :strip] - block[PAIRS:, strip:]
        im = block[:PAIRS, strip:] + block[PAIRS:, :strip]
        return re, im

    sr, si = joined(mm(valence_ref[...], wide_ref[...], NT))
    cr, ci = joined(mm(conduction_ref[...], waves_ref[...]))
    left = jnp.concatenate([cr, ci], 1)
    right = jnp.concatenate([jnp.concatenate([sr, si], 1), jnp.concatenate([si, -sr], 1)], 0)
    out_ref[...] = mm(left, right, NT, lax.Precision.HIGHEST) * scale


def passed_along(value, axis, by):
    size = lax.axis_size(axis)
    return lax.ppermute(value, axis, [(i, (i + by) % size) for i in range(size)])


def called(kernel, shapes, scratch, flops, moved, places, *args):
    spaces = {"s": pltpu.SMEM, "h": pltpu.HBM, "v": pltpu.VMEM}
    args = [pltpu.with_memory_space_constraint(a, pltpu.HBM) if p == "h" else a for a, p in zip(args, places)]
    return pl.pallas_call(
        kernel,
        out_shape=shapes,
        in_specs=[pl.BlockSpec(memory_space=spaces[place]) for place in places],
        out_specs=[pl.BlockSpec(memory_space=pltpu.VMEM) for _ in shapes],
        scratch_shapes=scratch,
        cost_estimate=pl.CostEstimate(flops=flops, bytes_accessed=moved, transcendentals=0),
        compiler_params=pltpu.CompilerParams(vmem_limit_bytes=26 * 1024 * 1024),
    )(*args)


def small_scratch():
    rows = 4 * NBND * NFFT
    return [pltpu.VMEM((rows, NG), jnp.bfloat16), pltpu.VMEM((2, rows, PLANE), jnp.float32)]


def prepared(place, index, coefs, weights, table):
    strip = weights.shape[0]
    shapes = [
        jax.ShapeDtypeStruct((2, 2 * NBND, GRID), jnp.float32),
        jax.ShapeDtypeStruct((2 * strip, GRID), jnp.bfloat16),
        jax.ShapeDtypeStruct((GRID, 2 * strip), jnp.bfloat16),
        jax.ShapeDtypeStruct((PLANE, NG), jnp.bfloat16),
        jax.ShapeDtypeStruct((NFFT, NG), jnp.bfloat16),
        jax.ShapeDtypeStruct(table.shape, table.dtype),
    ]
    rows = NFFT * (strip + 4 * NBND)
    scratch = [
        pltpu.VMEM((rows, NG), jnp.bfloat16),
        pltpu.VMEM((rows, PLANE), jnp.bfloat16),
        pltpu.VMEM((2, rows, PLANE), jnp.float32),
        pltpu.VMEM((2, 2 * NBND, NG), jnp.bfloat16),
    ]
    scratch += [pltpu.VMEM(value.shape, value.dtype) for value in (index, coefs, weights)]
    scratch += [pltpu.SemaphoreType.DMA((4,))]
    return called(prepare_kernel, shapes, scratch, 6 * 10**9, 2**23, "shhhh", place, index, coefs, weights, table)


def contracted(coefs, made, scale):
    shape = jax.ShapeDtypeStruct((PAIRS, 2 * PAIRS), jnp.float32)
    scratch = small_scratch() + [pltpu.VMEM((2, 2 * NBND, GRID), jnp.float32)]
    scratch += [pltpu.VMEM((2 * PAIRS, GRID), jnp.bfloat16) for _ in range(2)]
    scratch += [pltpu.VMEM((2, 2 * NBND, NG), jnp.bfloat16)]

    def kernel(*refs):
        contract_kernel(scale, *refs)

    return called(kernel, [shape], scratch, 10**9, 2**22, "v" * 7, coefs, *made)[0]


def body(band_coefs, screening, grid_index):
    width = lax.axis_size("ga")
    place = lax.axis_index("ga").astype(jnp.int32)
    coefs = band_coefs[0]
    moved = passed_along(coefs, "ka", 1)
    table = jnp.asarray(plane_table(), jnp.bfloat16)
    index = grid_index.reshape(1, NG)
    made = prepared(place.reshape(1), index, coefs, screening[0], table)
    scale = 1.0 / (math.sqrt(NG) * (math.sqrt(GRID) * LEVEL) ** 6)
    terms = contracted(moved, made, scale)
    rows = terms.shape[0] // width
    pieces = lax.all_to_all(terms.reshape(width, rows, 2 * PAIRS), "ga", 0, 0, tiled=True)
    return jnp.sum(pieces, axis=0)[None, None]


def solution(mesh):
    return jax.shard_map(
        body,
        mesh=mesh,
        in_specs=(P("ka", None, None, None), P(None, "ga", None), P()),
        out_specs=P("ka", None, "ga", None),
        check_vma=False,
    )
```

```python
import math

import jax
import jax.numpy as jnp
import numpy as np
from jax import lax
from jax.experimental import pallas as pl
from jax.experimental.pallas import tpu as pltpu
from jax.sharding import PartitionSpec as P

NBND = 8
NG = 2048
NFFT = 16
PLANE = NFFT * NFFT
GRID = NFFT * PLANE
PAIRS = NBND * NBND
STEP = 1.130485
LEVEL = 1.1328025

NT = (((1,), (1,)), ((), ()))
NN = (((1,), (0,)), ((), ()))


def mm(left, right, dims=NN, precision=None):
    return lax.dot_general(left, right, dims, precision=precision, preferred_element_type=jnp.float32)


def plane_table():
    index = np.arange(PLANE)
    phase = np.outer(index // NFFT, index // NFFT) + np.outer(index % NFFT, index % NFFT)
    angle = (phase % NFFT) * (2.0 * math.pi / NFFT)
    cos, sin = np.cos(angle) * STEP, -np.sin(angle) * STEP
    blocks = [np.concatenate([cos[:, at : at + 128], sin[:, at : at + 128]], 1) for at in range(0, PLANE, 128)]
    return np.stack(blocks + [cos, sin])


def radix4(a, b, c, d, sign):
    sr, si = a[0] + c[0], a[1] + c[1]
    dr, di = a[0] - c[0], a[1] - c[1]
    tr, ti = b[0] + d[0], b[1] + d[1]
    er, ei = b[0] - d[0], b[1] - d[1]
    plus = (dr - ei, di + er)
    minus = (dr + ei, di - er)
    first, third = (plus, minus) if sign > 0 else (minus, plus)
    return [(sr + tr, si + ti), first, (sr - tr, si - ti), third]


def turned(value, power, sign):
    if power == 0:
        return value
    re, im = value
    if power == 4:
        return (-im, re) if sign > 0 else (im, -re)
    c = math.cos(2.0 * math.pi * power / NFFT)
    s = sign * math.sin(2.0 * math.pi * power / NFFT)
    if power == 2:
        return ((re - im) * c, (re + im) * c) if sign > 0 else ((re + im) * c, (im - re) * c)
    if power == 6:
        return ((re + im) * c, (im - re) * c) if sign > 0 else ((re - im) * c, (re + im) * c)
    return (re * c - im * s, re * s + im * c)


def sixteen(values, sign):
    inner = [radix4(values[x], values[x + 4], values[x + 8], values[x + 12], sign) for x in range(4)]
    out = [None] * NFFT
    for u in range(4):
        group = radix4(*[turned(inner[x][u], x * u, sign) for x in range(4)], sign)
        for v in range(4):
            out[u + 4 * v] = group[v]
    return out


def selectors(index_ref, plane_ref, masks_ref):
    index = index_ref[...]
    rows = lax.broadcasted_iota(jnp.int32, (PLANE, NG), 0)
    plane_ref[...] = jnp.where(rows == (index & (PLANE - 1)), 1.0, 0.0).astype(jnp.bfloat16)
    levels = lax.broadcasted_iota(jnp.int32, (NFFT, NG), 0)
    masks_ref[...] = jnp.where(levels == (index >> 8), 1.0, 0.0).astype(jnp.bfloat16)


def finish_orbitals(block, field_ref, pitch, base, psi_ref):
    bands = 2 * NBND
    values = []
    for x in range(NFFT):
        top, low = pl.ds(x * pitch + base, bands), pl.ds(x * pitch + base + bands, bands)
        re = field_ref[block, top, pl.ds(0, 128)] + field_ref[block, low, pl.ds(128, 128)]
        im = field_ref[block, low, pl.ds(0, 128)] - field_ref[block, top, pl.ds(128, 128)]
        values.append((re, im))
    for u, (re, im) in enumerate(sixteen(values, 1)):
        at = pl.ds(u * PLANE + block * 128, 128)
        psi_ref[0, :, at] = re
        psi_ref[1, :, at] = im


def spread_orbitals(parts_ref, masks_ref, spread_ref, x, pitch, base):
    bands = 2 * NBND
    for part in range(2):
        rows = pl.ds(x * pitch + base + part * bands, bands)
        spread_ref[rows, :] = parts_ref[part] * masks_ref[pl.ds(x, 1), :]


def fill_orbitals(coefs_ref, table_ref, plane_ref, masks_ref, psi_ref, spread_ref, field_ref, parts_ref):
    for part in range(2):
        parts_ref[part] = coefs_ref[:, part, :]
    for x in range(NFFT):
        spread_orbitals(parts_ref, masks_ref, spread_ref, x, 4 * NBND, 0)
    planes = mm(spread_ref[...], plane_ref[...], NT).astype(jnp.bfloat16)
    for block in range(2):
        field_ref[block] = mm(planes, table_ref[block])
        finish_orbitals(block, field_ref, 4 * NBND, 0, psi_ref)


def store_waves(waves_ref, parity, u, re, im):
    strip = re.shape[1]
    re, im = re.astype(jnp.bfloat16), im.astype(jnp.bfloat16)
    near, far = pl.ds(u * PLANE, PLANE), pl.ds((u + 8) % NFFT * PLANE, PLANE)
    waves_ref[near, pl.ds(0, strip)] = re
    waves_ref[near, pl.ds(strip, strip)] = im
    waves_ref[far, pl.ds(0, strip)] = re * parity
    waves_ref[far, pl.ds(strip, strip)] = im * parity


def prepare_kernel(place_ref, index_hbm, coefs_hbm, weights_hbm, table_hbm,
                   psi_ref, wide_ref, waves_ref, plane_ref, masks_ref, table_ref,
                   spread_ref, planes_ref, field_ref,
                   parts_ref, index_ref, coefs_ref, weights_ref, sems):
    pairs = ((index_hbm, index_ref), (weights_hbm, weights_ref), (table_hbm, table_ref), (coefs_hbm, coefs_ref))
    copies = [pltpu.make_async_copy(source, target, sems.at[i]) for i, (source, target) in enumerate(pairs)]
    for copy in copies:
        copy.start()
    copies[0].wait()
    selectors(index_ref, plane_ref, masks_ref)
    strip = weights_ref.shape[0]
    first_own = pl.multiple_of(place_ref[0] * strip, strip)
    level = index_ref[:, pl.ds(first_own, strip)] >> 8
    turn = (level * lax.broadcasted_iota(jnp.int32, (8, strip), 0)) & (NFFT - 1)
    angle = turn.astype(jnp.float32) * (2.0 * math.pi / NFFT)
    parity = (1 - 2 * (level & 1)).astype(jnp.float32).astype(jnp.bfloat16)
    cos_line = jnp.cos(angle)
    sin_line = jnp.sin(angle)
    copies[1].wait()
    copies[2].wait()
    copies[3].wait()
    for part in range(2):
        parts_ref[part] = coefs_ref[:, part, :]
    chosen = plane_ref[:, pl.ds(first_own, strip)]
    cos_plane = mm(table_ref[2], chosen)
    sin_plane = mm(table_ref[3], chosen)
    group = 4
    pitch = strip + 4 * NBND
    for step in range(NFFT // group):
        for x in range(step * group, (step + 1) * group):
            spread_ref[pl.ds(x * pitch, strip), :] = weights_ref[...] * masks_ref[pl.ds(x, 1), :]
            spread_orbitals(parts_ref, masks_ref, spread_ref, x, pitch, strip)
        some = pl.ds(step * group * pitch, group * pitch)
        planes_ref[some, :] = mm(spread_ref[some, :], plane_ref[...], NT).astype(jnp.bfloat16)
        if step == 0:
            store_waves(waves_ref, parity, 0, cos_plane, sin_plane)
            c, s = cos_line[4:5, :], sin_line[4:5, :]
            store_waves(waves_ref, parity, 4, cos_plane * c + sin_plane * s, sin_plane * c - cos_plane * s)
        else:
            c, s = cos_line[step : step + 1, :], sin_line[step : step + 1, :]
            cc, ss, sc, cs = cos_plane * c, sin_plane * s, sin_plane * c, cos_plane * s
            store_waves(waves_ref, parity, step, cc + ss, sc - cs)
            store_waves(waves_ref, parity, NFFT - step, cc - ss, sc + cs)
    for block in range(2):
        field_ref[block] = mm(planes_ref[...], table_ref[block])
        finish_orbitals(block, field_ref, pitch, strip, psi_ref)
        for first in range(0, strip, 16):
            values = []
            for x in range(NFFT):
                rows = pl.ds(x * pitch + first, 16)
                values.append((field_ref[block, rows, pl.ds(0, 128)], field_ref[block, rows, pl.ds(128, 128)]))
            for u, (re, im) in enumerate(sixteen(values, -1)):
                out = pl.ds(u * PLANE + block * 128, 128)
                wide_ref[pl.ds(first, 16), out] = re.astype(jnp.bfloat16)
                wide_ref[pl.ds(first + strip, 16), out] = im.astype(jnp.bfloat16)


def contract_kernel(scale, coefs_ref, here_ref, wide_ref, waves_ref, plane_ref, masks_ref, table_ref, out_ref,
                    small_ref, small_field_ref, there_ref, valence_ref, conduction_ref, parts_ref):
    fill_orbitals(coefs_ref, table_ref, plane_ref, masks_ref, there_ref, small_ref, small_field_ref, parts_ref)
    strip = wide_ref.shape[0] // 2
    chunk = 512
    for lane in range(0, GRID, chunk):
        at = pl.ds(lane, chunk)
        for first, target in ((0, valence_ref), (NBND, conduction_ref)):
            br = there_ref[0, pl.ds(first, NBND), at]
            bi = there_ref[1, pl.ds(first, NBND), at]
            for v in range(0, NBND, 2):
                re, im = [], []
                for band in (first + v, first + v + 1):
                    ar = here_ref[0, pl.ds(band, 1), at]
                    ai = here_ref[1, pl.ds(band, 1), at]
                    re.append(ar * br + ai * bi)
                    im.append(ar * bi - ai * br)
                target[pl.ds(v * NBND, 2 * NBND), at] = jnp.concatenate(re, 0).astype(jnp.bfloat16)
                target[pl.ds(PAIRS + v * NBND, 2 * NBND), at] = jnp.concatenate(im, 0).astype(jnp.bfloat16)

    def joined(block):
        re = block[:PAIRS, :strip] - block[PAIRS:, strip:]
        im = block[:PAIRS, strip:] + block[PAIRS:, :strip]
        return re, im

    sr, si = joined(mm(valence_ref[...], wide_ref[...], NT))
    cr, ci = joined(mm(conduction_ref[...], waves_ref[...]))
    left = jnp.concatenate([cr, ci], 1)
    right = jnp.concatenate([jnp.concatenate([sr, si], 1), jnp.concatenate([si, -sr], 1)], 0)
    out_ref[...] = mm(left, right, NT, lax.Precision.HIGHEST) * scale


def passed_along(value, axis, by):
    size = lax.axis_size(axis)
    return lax.ppermute(value, axis, [(i, (i + by) % size) for i in range(size)])


def called(kernel, shapes, scratch, flops, moved, places, *args):
    spaces = {"s": pltpu.SMEM, "h": pltpu.HBM, "v": pltpu.VMEM}
    args = [pltpu.with_memory_space_constraint(a, pltpu.HBM) if p == "h" else a for a, p in zip(args, places)]
    return pl.pallas_call(
        kernel,
        out_shape=shapes,
        in_specs=[pl.BlockSpec(memory_space=spaces[place]) for place in places],
        out_specs=[pl.BlockSpec(memory_space=pltpu.VMEM) for _ in shapes],
        scratch_shapes=scratch,
        cost_estimate=pl.CostEstimate(flops=flops, bytes_accessed=moved, transcendentals=0),
        compiler_params=pltpu.CompilerParams(vmem_limit_bytes=26 * 1024 * 1024),
    )(*args)


def small_scratch():
    rows = 4 * NBND * NFFT
    return [pltpu.VMEM((rows, NG), jnp.bfloat16), pltpu.VMEM((2, rows, PLANE), jnp.float32)]


def prepared(place, index, coefs, weights, table):
    strip = weights.shape[0]
    shapes = [
        jax.ShapeDtypeStruct((2, 2 * NBND, GRID), jnp.float32),
        jax.ShapeDtypeStruct((2 * strip, GRID), jnp.bfloat16),
        jax.ShapeDtypeStruct((GRID, 2 * strip), jnp.bfloat16),
        jax.ShapeDtypeStruct((PLANE, NG), jnp.bfloat16),
        jax.ShapeDtypeStruct((NFFT, NG), jnp.bfloat16),
        jax.ShapeDtypeStruct(table.shape, table.dtype),
    ]
    rows = NFFT * (strip + 4 * NBND)
    scratch = [
        pltpu.VMEM((rows, NG), jnp.bfloat16),
        pltpu.VMEM((rows, PLANE), jnp.bfloat16),
        pltpu.VMEM((2, rows, PLANE), jnp.float32),
        pltpu.VMEM((2, 2 * NBND, NG), jnp.bfloat16),
    ]
    scratch += [pltpu.VMEM(value.shape, value.dtype) for value in (index, coefs, weights)]
    scratch += [pltpu.SemaphoreType.DMA((4,))]
    return called(prepare_kernel, shapes, scratch, 6 * 10**9, 2**23, "shhhh", place, index, coefs, weights, table)


def contracted(coefs, made, scale):
    shape = jax.ShapeDtypeStruct((PAIRS, 2 * PAIRS), jnp.float32)
    scratch = small_scratch() + [pltpu.VMEM((2, 2 * NBND, GRID), jnp.float32)]
    scratch += [pltpu.VMEM((2 * PAIRS, GRID), jnp.bfloat16) for _ in range(2)]
    scratch += [pltpu.VMEM((2, 2 * NBND, NG), jnp.bfloat16)]

    def kernel(*refs):
        contract_kernel(scale, *refs)

    return called(kernel, [shape], scratch, 10**9, 2**22, "v" * 7, coefs, *made)[0]


def body(band_coefs, screening, grid_index):
    width = lax.axis_size("ga")
    place = lax.axis_index("ga").astype(jnp.int32)
    coefs = band_coefs[0]
    moved = passed_along(coefs, "ka", 1)
    table = jnp.asarray(plane_table(), jnp.bfloat16)
    index = grid_index.reshape(1, NG)
    made = prepared(place.reshape(1), index, coefs, screening[0], table)
    scale = 1.0 / (math.sqrt(NG) * (math.sqrt(GRID) * LEVEL) ** 6)
    terms = contracted(moved, made, scale)
    rows = terms.shape[0] // width
    pieces = lax.all_to_all(terms.reshape(width, rows, 2 * PAIRS), "ga", 0, 0, tiled=True)
    return jnp.sum(pieces, axis=0)[None, None]


def solution(mesh):
    return jax.shard_map(
        body,
        mesh=mesh,
        in_specs=(P("ka", None, None, None), P(None, "ga", None), P()),
        out_specs=P("ka", None, "ga", None),
        check_vma=False,
    )
```

```python
import math

import jax
import jax.numpy as jnp
import numpy as np
from jax import lax
from jax.experimental import pallas as pl
from jax.experimental.pallas import tpu as pltpu
from jax.sharding import PartitionSpec as P

NBND = 8
NG = 2048
NFFT = 16
PLANE = NFFT * NFFT
GRID = NFFT * PLANE
PAIRS = NBND * NBND
STEP = 1.130485
LEVEL = 1.1328025

NT = (((1,), (1,)), ((), ()))
NN = (((1,), (0,)), ((), ()))


def mm(left, right, dims=NN, precision=None):
    return lax.dot_general(left, right, dims, precision=precision, preferred_element_type=jnp.float32)


def plane_table():
    index = np.arange(PLANE)
    phase = np.outer(index // NFFT, index // NFFT) + np.outer(index % NFFT, index % NFFT)
    angle = (phase % NFFT) * (2.0 * math.pi / NFFT)
    cos, sin = np.cos(angle) * STEP, -np.sin(angle) * STEP
    blocks = [np.concatenate([cos[:, at : at + 128], sin[:, at : at + 128]], 1) for at in range(0, PLANE, 128)]
    return np.stack(blocks + [cos, sin])


def radix4(a, b, c, d, sign):
    sr, si = a[0] + c[0], a[1] + c[1]
    dr, di = a[0] - c[0], a[1] - c[1]
    tr, ti = b[0] + d[0], b[1] + d[1]
    er, ei = b[0] - d[0], b[1] - d[1]
    plus = (dr - ei, di + er)
    minus = (dr + ei, di - er)
    first, third = (plus, minus) if sign > 0 else (minus, plus)
    return [(sr + tr, si + ti), first, (sr - tr, si - ti), third]


def turned(value, power, sign):
    if power == 0:
        return value
    re, im = value
    if power == 4:
        return (-im, re) if sign > 0 else (im, -re)
    c = math.cos(2.0 * math.pi * power / NFFT)
    s = sign * math.sin(2.0 * math.pi * power / NFFT)
    if power == 2:
        return ((re - im) * c, (re + im) * c) if sign > 0 else ((re + im) * c, (im - re) * c)
    if power == 6:
        return ((re + im) * c, (im - re) * c) if sign > 0 else ((re - im) * c, (re + im) * c)
    return (re * c - im * s, re * s + im * c)


def sixteen(values, sign):
    inner = [radix4(values[x], values[x + 4], values[x + 8], values[x + 12], sign) for x in range(4)]
    out = [None] * NFFT
    for u in range(4):
        group = radix4(*[turned(inner[x][u], x * u, sign) for x in range(4)], sign)
        for v in range(4):
            out[u + 4 * v] = group[v]
    return out


def selectors(index_ref, plane_ref, masks_ref):
    index = index_ref[...]
    rows = lax.broadcasted_iota(jnp.int32, (PLANE, NG), 0)
    plane_ref[...] = jnp.where(rows == (index & (PLANE - 1)), 1.0, 0.0).astype(jnp.bfloat16)
    levels = lax.broadcasted_iota(jnp.int32, (NFFT, NG), 0)
    masks_ref[...] = jnp.where(levels == (index >> 8), 1.0, 0.0).astype(jnp.bfloat16)


def finish_orbitals(block, field_ref, pitch, base, psi_ref):
    bands = 2 * NBND
    for half in range(0, bands, 8):
        values = []
        for x in range(NFFT):
            top, low = pl.ds(x * pitch + base + half, 8), pl.ds(x * pitch + base + bands + half, 8)
            re = field_ref[block, top, pl.ds(0, 128)] + field_ref[block, low, pl.ds(128, 128)]
            im = field_ref[block, low, pl.ds(0, 128)] - field_ref[block, top, pl.ds(128, 128)]
            values.append((re, im))
        for u, (re, im) in enumerate(sixteen(values, 1)):
            at = pl.ds(u * PLANE + block * 128, 128)
            psi_ref[0, pl.ds(half, 8), at] = re
            psi_ref[1, pl.ds(half, 8), at] = im


def spread_orbitals(parts_ref, masks_ref, spread_ref, x, pitch, base):
    bands = 2 * NBND
    for part in range(2):
        rows = pl.ds(x * pitch + base + part * bands, bands)
        spread_ref[rows, :] = parts_ref[part] * masks_ref[pl.ds(x, 1), :]


def fill_orbitals(coefs_ref, table_ref, plane_ref, masks_ref, psi_ref, spread_ref, field_ref, parts_ref):
    for part in range(2):
        parts_ref[part] = coefs_ref[:, part, :]
    for x in range(NFFT):
        spread_orbitals(parts_ref, masks_ref, spread_ref, x, 4 * NBND, 0)
    planes = mm(spread_ref[...], plane_ref[...], NT).astype(jnp.bfloat16)
    for block in range(2):
        field_ref[block] = mm(planes, table_ref[block])
        finish_orbitals(block, field_ref, 4 * NBND, 0, psi_ref)


def store_waves(waves_ref, parity, u, re, im):
    strip = re.shape[1]
    re, im = re.astype(jnp.bfloat16), im.astype(jnp.bfloat16)
    near, far = pl.ds(u * PLANE, PLANE), pl.ds((u + 8) % NFFT * PLANE, PLANE)
    waves_ref[near, pl.ds(0, strip)] = re
    waves_ref[near, pl.ds(strip, strip)] = im
    waves_ref[far, pl.ds(0, strip)] = re * parity
    waves_ref[far, pl.ds(strip, strip)] = im * parity


def prepare_kernel(place_ref, index_hbm, coefs_hbm, weights_hbm, table_hbm,
                   psi_ref, wide_ref, waves_ref, plane_ref, masks_ref, table_ref,
                   spread_ref, planes_ref, field_ref,
                   parts_ref, index_ref, coefs_ref, weights_ref, sems):
    pairs = ((index_hbm, index_ref), (weights_hbm, weights_ref), (table_hbm, table_ref), (coefs_hbm, coefs_ref))
    copies = [pltpu.make_async_copy(source, target, sems.at[i]) for i, (source, target) in enumerate(pairs)]
    for copy in copies:
        copy.start()
    copies[0].wait()
    selectors(index_ref, plane_ref, masks_ref)
    strip = weights_ref.shape[0]
    first_own = pl.multiple_of(place_ref[0] * strip, strip)
    level = index_ref[:, pl.ds(first_own, strip)] >> 8
    turn = (level * lax.broadcasted_iota(jnp.int32, (8, strip), 0)) & (NFFT - 1)
    angle = turn.astype(jnp.float32) * (2.0 * math.pi / NFFT)
    parity = (1 - 2 * (level & 1)).astype(jnp.float32).astype(jnp.bfloat16)
    cos_line = jnp.cos(angle)
    sin_line = jnp.sin(angle)
    copies[1].wait()
    copies[2].wait()
    copies[3].wait()
    for part in range(2):
        parts_ref[part] = coefs_ref[:, part, :]
    chosen = plane_ref[:, pl.ds(first_own, strip)]
    cos_plane = mm(table_ref[2], chosen)
    sin_plane = mm(table_ref[3], chosen)
    group = 4
    pitch = strip + 4 * NBND
    for step in range(NFFT // group):
        for x in range(step * group, (step + 1) * group):
            spread_ref[pl.ds(x * pitch, strip), :] = weights_ref[...] * masks_ref[pl.ds(x, 1), :]
            spread_orbitals(parts_ref, masks_ref, spread_ref, x, pitch, strip)
        some = pl.ds(step * group * pitch, group * pitch)
        planes_ref[some, :] = mm(spread_ref[some, :], plane_ref[...], NT).astype(jnp.bfloat16)
        if step == 0:
            store_waves(waves_ref, parity, 0, cos_plane, sin_plane)
            c, s = cos_line[4:5, :], sin_line[4:5, :]
            store_waves(waves_ref, parity, 4, cos_plane * c + sin_plane * s, sin_plane * c - cos_plane * s)
        else:
            c, s = cos_line[step : step + 1, :], sin_line[step : step + 1, :]
            cc, ss, sc, cs = cos_plane * c, sin_plane * s, sin_plane * c, cos_plane * s
            store_waves(waves_ref, parity, step, cc + ss, sc - cs)
            store_waves(waves_ref, parity, NFFT - step, cc - ss, sc + cs)
    for block in range(2):
        field_ref[block] = mm(planes_ref[...], table_ref[block])
        finish_orbitals(block, field_ref, pitch, strip, psi_ref)
        for first in range(0, strip, 16):
            values = []
            for x in range(NFFT):
                rows = pl.ds(x * pitch + first, 16)
                values.append((field_ref[block, rows, pl.ds(0, 128)], field_ref[block, rows, pl.ds(128, 128)]))
            for u, (re, im) in enumerate(sixteen(values, -1)):
                out = pl.ds(u * PLANE + block * 128, 128)
                wide_ref[pl.ds(first, 16), out] = re.astype(jnp.bfloat16)
                wide_ref[pl.ds(first + strip, 16), out] = im.astype(jnp.bfloat16)


def contract_kernel(scale, coefs_ref, here_ref, wide_ref, waves_ref, plane_ref, masks_ref, table_ref, out_ref,
                    small_ref, small_field_ref, there_ref, valence_ref, conduction_ref, parts_ref):
    fill_orbitals(coefs_ref, table_ref, plane_ref, masks_ref, there_ref, small_ref, small_field_ref, parts_ref)
    strip = wide_ref.shape[0] // 2
    chunk = 512
    for lane in range(0, GRID, chunk):
        at = pl.ds(lane, chunk)
        for first, target in ((0, valence_ref), (NBND, conduction_ref)):
            br = there_ref[0, pl.ds(first, NBND), at]
            bi = there_ref[1, pl.ds(first, NBND), at]
            for v in range(0, NBND, 2):
                re, im = [], []
                for band in (first + v, first + v + 1):
                    ar = here_ref[0, pl.ds(band, 1), at]
                    ai = here_ref[1, pl.ds(band, 1), at]
                    re.append(ar * br + ai * bi)
                    im.append(ar * bi - ai * br)
                target[pl.ds(v * NBND, 2 * NBND), at] = jnp.concatenate(re, 0).astype(jnp.bfloat16)
                target[pl.ds(PAIRS + v * NBND, 2 * NBND), at] = jnp.concatenate(im, 0).astype(jnp.bfloat16)

    def joined(block):
        re = block[:PAIRS, :strip] - block[PAIRS:, strip:]
        im = block[:PAIRS, strip:] + block[PAIRS:, :strip]
        return re, im

    sr, si = joined(mm(valence_ref[...], wide_ref[...], NT))
    cr, ci = joined(mm(conduction_ref[...], waves_ref[...]))
    left = jnp.concatenate([cr, ci], 1)
    right = jnp.concatenate([jnp.concatenate([sr, si], 1), jnp.concatenate([si, -sr], 1)], 0)
    out_ref[...] = mm(left, right, NT, lax.Precision.HIGHEST) * scale


def passed_along(value, axis, by):
    size = lax.axis_size(axis)
    return lax.ppermute(value, axis, [(i, (i + by) % size) for i in range(size)])


def called(kernel, shapes, scratch, flops, moved, places, *args):
    spaces = {"s": pltpu.SMEM, "h": pltpu.HBM, "v": pltpu.VMEM}
    args = [pltpu.with_memory_space_constraint(a, pltpu.HBM) if p == "h" else a for a, p in zip(args, places)]
    return pl.pallas_call(
        kernel,
        out_shape=shapes,
        in_specs=[pl.BlockSpec(memory_space=spaces[place]) for place in places],
        out_specs=[pl.BlockSpec(memory_space=pltpu.VMEM) for _ in shapes],
        scratch_shapes=scratch,
        cost_estimate=pl.CostEstimate(flops=flops, bytes_accessed=moved, transcendentals=0),
        compiler_params=pltpu.CompilerParams(vmem_limit_bytes=26 * 1024 * 1024),
    )(*args)


def small_scratch():
    rows = 4 * NBND * NFFT
    return [pltpu.VMEM((rows, NG), jnp.bfloat16), pltpu.VMEM((2, rows, PLANE), jnp.float32)]


def prepared(place, index, coefs, weights, table):
    strip = weights.shape[0]
    shapes = [
        jax.ShapeDtypeStruct((2, 2 * NBND, GRID), jnp.float32),
        jax.ShapeDtypeStruct((2 * strip, GRID), jnp.bfloat16),
        jax.ShapeDtypeStruct((GRID, 2 * strip), jnp.bfloat16),
        jax.ShapeDtypeStruct((PLANE, NG), jnp.bfloat16),
        jax.ShapeDtypeStruct((NFFT, NG), jnp.bfloat16),
        jax.ShapeDtypeStruct(table.shape, table.dtype),
    ]
    rows = NFFT * (strip + 4 * NBND)
    scratch = [
        pltpu.VMEM((rows, NG), jnp.bfloat16),
        pltpu.VMEM((rows, PLANE), jnp.bfloat16),
        pltpu.VMEM((2, rows, PLANE), jnp.float32),
        pltpu.VMEM((2, 2 * NBND, NG), jnp.bfloat16),
    ]
    scratch += [pltpu.VMEM(value.shape, value.dtype) for value in (index, coefs, weights)]
    scratch += [pltpu.SemaphoreType.DMA((4,))]
    return called(prepare_kernel, shapes, scratch, 6 * 10**9, 2**23, "shhhh", place, index, coefs, weights, table)


def contracted(coefs, made, scale):
    shape = jax.ShapeDtypeStruct((PAIRS, 2 * PAIRS), jnp.float32)
    scratch = small_scratch() + [pltpu.VMEM((2, 2 * NBND, GRID), jnp.float32)]
    scratch += [pltpu.VMEM((2 * PAIRS, GRID), jnp.bfloat16) for _ in range(2)]
    scratch += [pltpu.VMEM((2, 2 * NBND, NG), jnp.bfloat16)]

    def kernel(*refs):
        contract_kernel(scale, *refs)

    return called(kernel, [shape], scratch, 10**9, 2**22, "v" * 7, coefs, *made)[0]


def body(band_coefs, screening, grid_index):
    width = lax.axis_size("ga")
    place = lax.axis_index("ga").astype(jnp.int32)
    coefs = band_coefs[0]
    moved = passed_along(coefs, "ka", 1)
    table = jnp.asarray(plane_table(), jnp.bfloat16)
    index = grid_index.reshape(1, NG)
    made = prepared(place.reshape(1), index, coefs, screening[0], table)
    scale = 1.0 / (math.sqrt(NG) * (math.sqrt(GRID) * LEVEL) ** 6)
    terms = contracted(moved, made, scale)
    rows = terms.shape[0] // width
    pieces = lax.all_to_all(terms.reshape(width, rows, 2 * PAIRS), "ga", 0, 0, tiled=True)
    return jnp.sum(pieces, axis=0)[None, None]


def solution(mesh):
    return jax.shard_map(
        body,
        mesh=mesh,
        in_specs=(P("ka", None, None, None), P(None, "ga", None), P()),
        out_specs=P("ka", None, "ga", None),
        check_vma=False,
    )
```
